128 devices in a mesh: chan: 16 (over z, x), mode: 8 (over y, core).
Axes of the slice: x: 4, y: 4, z: 4, core: 2. Of those that a mesh axis runs over, the one named last changes fastest.
Arguments:
- weight: bfloat16 [512, 2, 32, 32, 256], P('chan', None, 'mode'), may hold values from -0.59765625 to 0.59765625
- gradient: bfloat16 [512, 2, 32, 32, 256], P('chan', None, 'mode'), may hold values from -6 to 6
- first_moment: float32 [128, 2, 16, 16, 128], P('chan', None, None, 'mode'), may hold values from -2 to 2
- second_moment: float32 [128, 2, 16, 16, 128], P('chan', None, None, 'mode'), may hold values from 0.0005 to 0.02
- u_in: float32 [512, 128], P('chan'), may hold values from -0.25 to 0.25
- u_out: bfloat16 [256, 128], replicated, may hold values from -0.375 to 0.375
- u_modes_a: float32 [32, 16], replicated, may hold values from -1 to 1
- u_modes_b: float32 [32, 16], replicated, may hold values from -1 to 1
Outputs:
- new_weight: bfloat16 [512, 2, 32, 32, 256], P('chan', None, 'mode')
- new_first: float32 [128, 2, 16, 16, 128], P('chan', None, None, 'mode')
- new_second: float32 [128, 2, 16, 16, 128], P('chan', None, None, 'mode')
The draws below stay inside these ranges and needn't reach their ends.
All inputs are finite; a program needn't handle non-finite values.
Results may differ from the reference program's by a relative error of at most 0.004.
Values sent between devices are 32-bit elements; how exact they have to be, the bound alone decides.
No kernel may reach another device: no remote copies, remote signals or barrier semaphores. Data moves between devices by JAX's collectives and lax.ppermute only.
A program may use at most 128 MiB of HBM per device.

```python
import math
import jax
import jax.numpy as jnp
from jax import lax

IN_CH = 512
OUT_CH = 256
MODES_A = 32
MODES_B = 32
RANK_IN = 128
RANK_OUT = 128
RANK_A = 16
RANK_B = 16
STEP = 4


def levels(own_key, shape, cuts, low, largest):
    gain = 1.0
    for dim, shards_of in cuts:
        steps = jax.random.uniform(jax.random.fold_in(jax.random.fold_in(own_key, 6), dim), (shards_of,), jnp.float32, low / len(cuts), largest / len(cuts))
        gain = gain * jnp.repeat(jnp.exp(steps), shape[dim] // shards_of).reshape((-1,) + (1,) * (len(shape) - 1 - dim))
    return gain


def normal_values(key, shape, scale, most, shards=(), dtype=jnp.bfloat16):
    result = jax.random.normal(key, shape, jnp.float32) * scale
    if len(shards) > 0:
        result = levels(key, shape, shards, -0.22, 0.18) * result
    return jnp.clip(result, min=-most, max=most).astype(dtype)


def setup_inputs(seed: int = 0) -> dict:
    key_list = jax.random.split(jax.random.key(seed), 9)
    return {
        "weight": normal_values(key_list[0], (IN_CH, 2, MODES_A, MODES_B, OUT_CH), 0.1, 0.59765625, ((0, 16), (2, 8))),
        "gradient": normal_values(key_list[1], (IN_CH, 2, MODES_A, MODES_B, OUT_CH), 1.0, 6.0, ((0, 16), (2, 8))),
        "first_moment": normal_values(key_list[2], (RANK_IN, 2, RANK_A, RANK_B, RANK_OUT), 0.3, 2.0, ((0, 16), (3, 8)), jnp.float32),
        "second_moment": jnp.clip(jnp.exp(math.log(0.02) - 3.6888794 * jax.random.uniform(key_list[3], (RANK_IN, 2, RANK_A, RANK_B, RANK_OUT), jnp.float32) ** levels(key_list[3], (RANK_IN, 2, RANK_A, RANK_B, RANK_OUT), ((0, 16), (3, 8)), -0.2, 0.2)), 0.0005, 0.02),
        "u_in": normal_values(key_list[4], (IN_CH, RANK_IN), IN_CH ** -0.5, 0.25, ((0, 16),), jnp.float32),
        "u_out": normal_values(key_list[5], (OUT_CH, RANK_OUT), OUT_CH ** -0.5, 0.375),
        "u_modes_a": normal_values(key_list[6], (MODES_A, RANK_A), MODES_A ** -0.5, 1.0, (), jnp.float32),
        "u_modes_b": normal_values(key_list[7], (MODES_B, RANK_B), MODES_B ** -0.5, 1.0, (), jnp.float32),
    }


HIGH = lax.Precision.HIGHEST
beta_one = 0.9
beta_two = 0.999
step_rate = 0.5

def reference(weight, gradient, first_moment, second_moment, u_in, u_out, u_modes_a, u_modes_b):
    rows = math.gcd(IN_CH, 64)
    nblocks = IN_CH // rows
    grad_blocks = gradient.reshape(nblocks, rows, 2, MODES_A, MODES_B, OUT_CH)
    weight_blocks = weight.reshape(nblocks, rows, 2, MODES_A, MODES_B, OUT_CH)
    factor_blocks = u_in.reshape(nblocks, rows, RANK_IN)

    def project(carry, pair):
        block, factor = pair
        reduced = jnp.dot(block.reshape(-1, OUT_CH), u_out, preferred_element_type=jnp.float32)
        reduced = reduced.reshape(rows, 2, MODES_A, MODES_B, RANK_OUT)
        narrowed = jnp.einsum('ipabo,bs->ipaso', reduced, u_modes_b, precision=HIGH)
        mixed = jnp.einsum('ipaso,ar->iprso', narrowed, u_modes_a, precision=HIGH)
        return (carry + jnp.einsum('ik,iprso->kprso', factor, mixed, precision=HIGH), None)
    start = jnp.zeros((RANK_IN, 2, RANK_A, RANK_B, RANK_OUT), jnp.float32)
    core, unused = lax.scan(project, start, (grad_blocks, factor_blocks))
    new_first = beta_one * first_moment + (1.0 - beta_one) * core
    new_second = beta_two * second_moment + (1.0 - beta_two) * core * core
    direction = new_first / (1.0 - beta_one ** STEP) / (jnp.sqrt(new_second / (1.0 - beta_two ** STEP)) + 1e-08)

    def restore(pair):
        block, factor = pair
        spread = jnp.einsum('ik,kprso->iprso', factor, direction, precision=HIGH)
        wide = jnp.einsum('iprso,ar->ipaso', spread, u_modes_a, precision=HIGH)
        expanded = jnp.einsum('ipaso,bs->ipabo', wide, u_modes_b, precision=HIGH).astype(jnp.bfloat16)
        update = jnp.dot(expanded.reshape(-1, RANK_OUT), u_out.T, preferred_element_type=jnp.float32)
        update = update.reshape(rows, 2, MODES_A, MODES_B, OUT_CH)
        return (block.astype(jnp.float32) - step_rate * update).astype(jnp.bfloat16)
    new_weight = lax.map(restore, (weight_blocks, factor_blocks)).reshape(weight.shape)
    return (new_weight, new_first, new_second)
```

```python
import jax
import jax.numpy as jnp
from jax import lax
from jax.experimental import pallas as pl
from jax.experimental.pallas import tpu as pltpu
from jax.sharding import PartitionSpec as P


STEP = 4
beta_one = 0.9
beta_two = 0.999
step_rate = 0.5

F32 = jnp.float32
BF16 = jnp.bfloat16
VMEM_LIMIT = 24 * 1024 * 1024
VMEM = pl.BlockSpec(memory_space=pltpu.VMEM)


def dot(a, b, dims=((1,), (0,))):
    return lax.dot_general(a, b, (dims, ((), ())), preferred_element_type=F32)


def split(x):
    hi = x.astype(BF16)
    return hi, (x - hi.astype(F32)).astype(BF16)


def dot3(a, b, dims=((1,), (0,))):
    return dot(a[0], b[0], dims) + (dot(a[0], b[1], dims) + dot(a[1], b[0], dims))


def swap_groups(tiles):
    lane = lax.broadcasted_iota(jnp.int32, tiles[0].shape, tiles[0].ndim - 1)
    axis = tiles[0].ndim - 1
    for bit in (1, 2, 4):
        upper = (lane & (16 * bit)) != 0
        out = list(tiles)
        for x in range(8):
            if x & bit:
                continue
            low, high = tiles[x], tiles[x + bit]
            out[x] = jnp.where(upper, pltpu.roll(high, 16 * bit, axis), low)
            out[x + bit] = jnp.where(upper, high, pltpu.roll(low, 128 - 16 * bit, axis))
        tiles = out
    return tiles


def one_hot(shape, row_of, col_of):
    rows = lax.broadcasted_iota(jnp.int32, shape, 0)
    cols = lax.broadcasted_iota(jnp.int32, shape, 1)
    return row_of(rows) == col_of(cols)


def spread_b(ub_t):
    rows = one_hot((128, 16), lambda r: r // 8, lambda c: c).astype(BF16)
    cols = one_hot((32, 256), lambda r: r, lambda c: c % 32).astype(BF16)
    same = one_hot((128, 256), lambda r: r % 8, lambda c: c // 32)
    return [
        jnp.where(same, dot(dot(rows, part).astype(BF16), cols), 0.0).astype(BF16)
        for part in split(ub_t)
    ]


def head_kernel(g_ref, uo_ref, ubt_ref, z_ref, kb_ref):
    @pl.when(pl.program_id(0) == 0)
    def _():
        hi, lo = spread_b(ubt_ref[...])
        kb_ref[0:128, :] = hi
        kb_ref[128:256, :] = lo

    kb = kb_ref[...]
    uo = uo_ref[...]
    for p in range(2):
        tiles = []
        for a in range(4):
            both = dot(kb, g_ref[:, p, a].reshape(256, 256))
            hi, lo = split(both[0:128] + both[128:256])
            nar = (dot(hi, uo) + dot(lo, uo)).reshape(8, 2, 8, 128)
            tiles += [nar[:, 0].reshape(64, 128), nar[:, 1].reshape(64, 128)]
        tiles = swap_groups(tiles)
        for j in range(8):
            z_ref[p * 8 + j] = tiles[j].reshape(8, 8, 128)


def head(gradient, u_out, ub_t):
    return pl.pallas_call(
        head_kernel,
        grid=(4,),
        in_specs=[
            pl.BlockSpec((8, 2, 4, 32, 256), lambda g: (g, 0, 0, 0, 0)),
            pl.BlockSpec((256, 128), lambda g: (0, 0)),
            pl.BlockSpec((16, 32), lambda g: (0, 0)),
        ],
        out_specs=pl.BlockSpec((16, 8, 8, 128), lambda g: (0, 0, g, 0)),
        out_shape=jax.ShapeDtypeStruct((16, 8, 32, 128), F32),
        scratch_shapes=[pltpu.VMEM((256, 256), BF16)],
        compiler_params=pltpu.CompilerParams(vmem_limit_bytes=54 * 1024 * 1024),
        name="head",
    )(gradient, u_out, ub_t)


def place(c, other):
    return (other // 4 + 4 - c // 4) % 4, (other % 4 + 4 - c % 4) % 4


def pack_kernel(fm_ref, sm_ref, ui_ref, o_ref):
    me = lax.axis_index("chan")
    for p in range(2):
        tiles = {}
        for which, ref in enumerate((fm_ref, sm_ref)):
            for q in range(4):
                tiles[which, q] = swap_groups([ref[:, p, q * 8 + x, :] for x in range(8)])
        for j in range(8):
            dz, dx = place(me, p * 8 + j)
            for which in range(2):
                for q in range(4):
                    at = which * 32 + q * 8
                    o_ref[dz, dx, at : at + 8, :] = tiles[which, q][j]
            o_ref[dz, dx, 64:96, :] = ui_ref[...]


def pack(fm, sm, u_in):
    return pl.pallas_call(
        pack_kernel,
        out_shape=jax.ShapeDtypeStruct((4, 4, 96, 128), F32),
        compiler_params=pltpu.CompilerParams(vmem_limit_bytes=VMEM_LIMIT),
        name="pack",
    )(fm, sm, u_in)


def exchange(blocks):
    rows = [blocks[0]]
    for d in range(1, 4):
        ring = [(c, (c // 4 + d) % 4 * 4 + c % 4) for c in range(16)]
        rows.append(lax.ppermute(blocks[d], "chan", ring))
    rows = jnp.stack(rows, axis=1)
    columns = [rows[0]]
    for d in range(1, 4):
        ring = [(c, c // 4 * 4 + (c % 4 + d) % 4) for c in range(16)]
        columns.append(lax.ppermute(rows[d], "chan", ring))
    return jnp.stack(columns)


def adam(core, fm, sm):
    new_first = beta_one * fm + (1.0 - beta_one) * core
    new_second = beta_two * sm + (1.0 - beta_two) * core * core
    return new_first, new_second


def prep_kernel(ua_ref, uat_ref, ka_ref, kat_ref):
    tall = one_hot((1024, 32), lambda r: r // 32, lambda c: c).astype(BF16)
    wide = one_hot((16, 512), lambda r: r, lambda c: c // 32).astype(BF16)
    same = one_hot((1024, 512), lambda r: r % 32, lambda c: c % 32)
    for n, part in enumerate(split(ua_ref[...])):
        ka_ref[n] = jnp.where(same, dot(dot(tall, part).astype(BF16), wide), 0.0).astype(BF16)
    tall = one_hot((512, 16), lambda r: r // 32, lambda c: c).astype(BF16)
    wide = one_hot((32, 1024), lambda r: r, lambda c: c // 32).astype(BF16)
    same = one_hot((512, 1024), lambda r: r % 32, lambda c: c % 32)
    for n, part in enumerate(split(uat_ref[...])):
        kat_ref[n] = jnp.where(same, dot(dot(tall, part).astype(BF16), wide), 0.0).astype(BF16)


def prep(u_a, u_at):
    return pl.pallas_call(
        prep_kernel,
        out_shape=(
            jax.ShapeDtypeStruct((2, 1024, 512), BF16),
            jax.ShapeDtypeStruct((2, 512, 1024), BF16),
        ),
        in_specs=[VMEM] * 2,
        out_specs=(VMEM, VMEM),
        compiler_params=pltpu.CompilerParams(vmem_limit_bytes=VMEM_LIMIT),
        name="prep",
    )(u_a, u_at)


def mid_kernel(x_ref, pk_ref, ka_ref, kat_ref, w_ref, core_ref):
    me = lax.axis_index("chan")

    def gathered(at, rows):
        parts = []
        for c in range(16):
            dz, dx = place(c, me)
            parts.append(pk_ref[dx, dz, at : at + rows, :])
        return jnp.concatenate(parts, axis=0)

    ui = gathered(64, 32)
    uit = split(ui.T)
    ui = split(ui)
    part = [dot3(uit, split(x_ref[:, m].reshape(512, 128))) for m in range(8)]
    part = split(jnp.concatenate(part, axis=1))
    core = dot3(part, (ka_ref[0], ka_ref[1]))
    dirs = []
    for q in range(4):
        mine = core[:, q * 128 : q * 128 + 128]
        for c in range(16):
            dz, dx = place(me, c)
            core_ref[dz, dx, q * 8 : q * 8 + 8, :] = mine[c * 8 : c * 8 + 8]
        new_first, new_second = adam(mine, gathered(q * 8, 8), gathered(32 + q * 8, 8))
        dirs.append(
            new_first / (1.0 - beta_one**STEP) / (jnp.sqrt(new_second / (1.0 - beta_two**STEP)) + 1e-08)
        )
    back = dot3(split(jnp.concatenate(dirs, axis=1)), (kat_ref[0], kat_ref[1]))
    for m in range(8):
        wide = dot3(ui, split(back[:, m * 128 : m * 128 + 128]))
        w_ref[:, m] = wide.reshape(16, 32, 128)


def mid(x, packed, ka, kat):
    return pl.pallas_call(
        mid_kernel,
        out_shape=(
            jax.ShapeDtypeStruct((16, 8, 32, 128), F32),
            jax.ShapeDtypeStruct((4, 4, 32, 128), F32),
        ),
        in_specs=[VMEM] * 4,
        out_specs=(VMEM, VMEM),
        compiler_params=pltpu.CompilerParams(vmem_limit_bytes=VMEM_LIMIT),
        name="mid",
    )(x, packed, ka, kat)


def moments_kernel(c_ref, fm_ref, sm_ref, nf_ref, ns_ref):
    me = lax.axis_index("chan")
    for p in range(2):
        at = [place(p * 8 + j, me) for j in range(8)]
        for q in range(4):
            tiles = swap_groups([c_ref[dx, dz, q * 8 : q * 8 + 8, :] for dz, dx in at])
            for x in range(8):
                s = q * 8 + x
                new_first, new_second = adam(tiles[x], fm_ref[:, p, s, :], sm_ref[:, p, s, :])
                nf_ref[:, p, s, :] = new_first
                ns_ref[:, p, s, :] = new_second


def moments(core, fm, sm):
    return pl.pallas_call(
        moments_kernel,
        out_shape=(jax.ShapeDtypeStruct(fm.shape, F32), jax.ShapeDtypeStruct(sm.shape, F32)),
        compiler_params=pltpu.CompilerParams(vmem_limit_bytes=VMEM_LIMIT),
        name="moments",
    )(core, fm, sm)


def tail_kernel(v_ref, w_ref, uo_ref, ubt_ref, o_ref, kb_ref):
    @pl.when(pl.program_id(0) == 0)
    def _():
        hi, lo = spread_b(ubt_ref[...])
        kb_ref[0] = hi.T
        kb_ref[1] = lo.T

    kb = (kb_ref[0], kb_ref[1])
    uo = uo_ref[...]
    rows = pl.ds(pl.program_id(0) * 8, 8)
    for p in range(2):
        tiles = swap_groups([v_ref[p * 8 + j, :, rows, :].reshape(64, 128) for j in range(8)])
        for a in range(4):
            wide = jnp.stack([t.reshape(8, 8, 128) for t in tiles[2 * a : 2 * a + 2]], axis=1)
            expanded = dot3(kb, split(wide.reshape(128, 128))).astype(BF16)
            update = dot(expanded, uo, ((1,), (1,))).reshape(8, 32, 256)
            o_ref[:, p, a] = (w_ref[:, p, a].astype(F32) - step_rate * update).astype(BF16)


def tail(v, weight, u_out, ub_t):
    return pl.pallas_call(
        tail_kernel,
        grid=(4,),
        in_specs=[
            VMEM,
            pl.BlockSpec((8, 2, 4, 32, 256), lambda g: (g, 0, 0, 0, 0)),
            pl.BlockSpec((256, 128), lambda g: (0, 0)),
            pl.BlockSpec((16, 32), lambda g: (0, 0)),
        ],
        out_specs=pl.BlockSpec((8, 2, 4, 32, 256), lambda g: (g, 0, 0, 0, 0)),
        out_shape=jax.ShapeDtypeStruct((32, 2, 4, 32, 256), BF16),
        scratch_shapes=[pltpu.VMEM((2, 256, 128), BF16)],
        compiler_params=pltpu.CompilerParams(vmem_limit_bytes=54 * 1024 * 1024),
        name="tail",
    )(v, weight, u_out, ub_t)


def shards(weight, gradient, first_moment, second_moment, u_in, u_out, u_modes_a, u_modes_b):
    both = ("chan", "mode")
    ub_t = u_modes_b.T
    fm = first_moment.reshape(8, 2, 32, 128)
    sm = second_moment.reshape(8, 2, 32, 128)
    sent = head(gradient, u_out, ub_t).reshape(128, 32, 128)
    got = lax.all_to_all(sent, both, 0, 0, tiled=True).reshape(16, 8, 32, 128)
    packed = exchange(pack(fm, sm, u_in))
    ka, kat = prep(u_modes_a, u_modes_a.T)
    wide, core = mid(got, packed, ka, kat)
    wide = lax.all_to_all(wide.reshape(128, 32, 128), both, 0, 0, tiled=True)
    core = exchange(core)
    new_first, new_second = moments(core, fm, sm)
    new_weight = tail(wide.reshape(16, 8, 32, 128), weight, u_out, ub_t)
    return new_weight, new_first.reshape(first_moment.shape), new_second.reshape(second_moment.shape)


def solution(mesh):
    in_specs = (
        P("chan", None, "mode", None, None),
        P("chan", None, "mode", None, None),
        P("chan", None, None, "mode", None),
        P("chan", None, None, "mode", None),
        P("chan", None),
        P(),
        P(),
        P(),
    )
    out_specs = (
        P("chan", None, "mode", None, None),
        P("chan", None, None, "mode", None),
        P("chan", None, None, "mode", None),
    )
    return jax.shard_map(shards, mesh=mesh, in_specs=in_specs, out_specs=out_specs, check_vma=False)
```

```python
import jax
import jax.numpy as jnp
from jax import lax
from jax.experimental import pallas as pl
from jax.experimental.pallas import tpu as pltpu
from jax.sharding import PartitionSpec as P


STEP = 4
beta_one = 0.9
beta_two = 0.999
step_rate = 0.5

F32 = jnp.float32
BF16 = jnp.bfloat16
VMEM_LIMIT = 24 * 1024 * 1024
VMEM = pl.BlockSpec(memory_space=pltpu.VMEM)
HBM = pl.BlockSpec(memory_space=pltpu.HBM)


def dot(a, b, dims=((1,), (0,))):
    return lax.dot_general(a, b, (dims, ((), ())), preferred_element_type=F32)


def split(x):
    hi = x.astype(BF16)
    return hi, (x - hi.astype(F32)).astype(BF16)


def dot3(a, b, dims=((1,), (0,))):
    return dot(a[0], b[0], dims) + (dot(a[0], b[1], dims) + dot(a[1], b[0], dims))


def swap_groups(tiles):
    lane = lax.broadcasted_iota(jnp.int32, tiles[0].shape, tiles[0].ndim - 1)
    axis = tiles[0].ndim - 1
    for bit in (1, 2, 4):
        upper = (lane & (16 * bit)) != 0
        out = list(tiles)
        for x in range(8):
            if x & bit:
                continue
            low, high = tiles[x], tiles[x + bit]
            out[x] = jnp.where(upper, pltpu.roll(high, 16 * bit, axis), low)
            out[x + bit] = jnp.where(upper, high, pltpu.roll(low, 128 - 16 * bit, axis))
        tiles = out
    return tiles


def one_hot(shape, row_of, col_of):
    rows = lax.broadcasted_iota(jnp.int32, shape, 0)
    cols = lax.broadcasted_iota(jnp.int32, shape, 1)
    return row_of(rows) == col_of(cols)


def spread_b(ub_t):
    rows = one_hot((128, 16), lambda r: r // 8, lambda c: c).astype(BF16)
    cols = one_hot((32, 256), lambda r: r, lambda c: c % 32).astype(BF16)
    same = one_hot((128, 256), lambda r: r % 8, lambda c: c // 32)
    return [
        jnp.where(same, dot(dot(rows, part).astype(BF16), cols), 0.0).astype(BF16)
        for part in split(ub_t)
    ]


def head_kernel(g_ref, uo_ref, ubt_ref, z_ref, kb_ref):
    @pl.when(pl.program_id(0) == 0)
    def _():
        hi, lo = spread_b(ubt_ref[...])
        kb_ref[0:128, :] = hi
        kb_ref[128:256, :] = lo

    kb = kb_ref[...]
    uo = uo_ref[...]
    for p in range(2):
        tiles = []
        for a in range(4):
            both = dot(kb, g_ref[:, p, a].reshape(256, 256))
            hi, lo = split(both[0:128] + both[128:256])
            nar = (dot(hi, uo) + dot(lo, uo)).reshape(8, 2, 8, 128)
            tiles += [nar[:, 0].reshape(64, 128), nar[:, 1].reshape(64, 128)]
        tiles = swap_groups(tiles)
        for j in range(8):
            z_ref[p * 8 + j] = tiles[j].reshape(8, 8, 128)


def head(gradient, u_out, ub_t):
    return pl.pallas_call(
        head_kernel,
        grid=(4,),
        in_specs=[
            pl.BlockSpec((8, 2, 4, 32, 256), lambda g: (g, 0, 0, 0, 0)),
            pl.BlockSpec((256, 128), lambda g: (0, 0)),
            pl.BlockSpec((16, 32), lambda g: (0, 0)),
        ],
        out_specs=pl.BlockSpec((16, 8, 8, 128), lambda g: (0, 0, g, 0)),
        out_shape=jax.ShapeDtypeStruct((16, 8, 32, 128), F32),
        scratch_shapes=[pltpu.VMEM((256, 256), BF16)],
        compiler_params=pltpu.CompilerParams(vmem_limit_bytes=54 * 1024 * 1024),
        name="head",
    )(gradient, u_out, ub_t)


def place(c, other):
    return (other // 4 + 4 - c // 4) % 4, (other % 4 + 4 - c % 4) % 4


def pack_kernel(fm_ref, sm_ref, ui_ref, after_ref, o_ref):
    me = lax.axis_index("chan")
    for p in range(2):
        tiles = {}
        for which, ref in enumerate((fm_ref, sm_ref)):
            for q in range(4):
                tiles[which, q] = swap_groups([ref[:, p, q * 8 + x, :] for x in range(8)])
        for j in range(8):
            dz, dx = place(me, p * 8 + j)
            for which in range(2):
                for q in range(4):
                    at = which * 32 + q * 8
                    o_ref[dz, dx, at : at + 8, :] = tiles[which, q][j]
            o_ref[dz, dx, 64:96, :] = ui_ref[...]


def pack(fm, sm, u_in, after):
    return pl.pallas_call(
        pack_kernel,
        in_specs=[VMEM, VMEM, VMEM, HBM],
        out_specs=VMEM,
        out_shape=jax.ShapeDtypeStruct((4, 4, 96, 128), F32),
        compiler_params=pltpu.CompilerParams(vmem_limit_bytes=VMEM_LIMIT),
        name="pack",
    )(fm, sm, u_in, after)


def exchange(blocks):
    rows = [blocks[0]]
    for d in range(1, 4):
        ring = [(c, (c // 4 + d) % 4 * 4 + c % 4) for c in range(16)]
        rows.append(lax.ppermute(blocks[d], "chan", ring))
    rows = jnp.stack(rows, axis=1)
    columns = [rows[0]]
    for d in range(1, 4):
        ring = [(c, c // 4 * 4 + (c % 4 + d) % 4) for c in range(16)]
        columns.append(lax.ppermute(rows[d], "chan", ring))
    return jnp.stack(columns)


def adam(core, fm, sm):
    new_first = beta_one * fm + (1.0 - beta_one) * core
    new_second = beta_two * sm + (1.0 - beta_two) * core * core
    return new_first, new_second


def prep_kernel(ua_ref, uat_ref, ka_hbm, kat_hbm, ka_ref, kat_ref, sems):
    tall = one_hot((1024, 32), lambda r: r // 32, lambda c: c).astype(BF16)
    wide = one_hot((16, 512), lambda r: r, lambda c: c // 32).astype(BF16)
    same = one_hot((1024, 512), lambda r: r % 32, lambda c: c % 32)
    for n, part in enumerate(split(ua_ref[...])):
        ka_ref[n] = jnp.where(same, dot(dot(tall, part).astype(BF16), wide), 0.0).astype(BF16)
    tall = one_hot((512, 16), lambda r: r // 32, lambda c: c).astype(BF16)
    wide = one_hot((32, 1024), lambda r: r, lambda c: c // 32).astype(BF16)
    same = one_hot((512, 1024), lambda r: r % 32, lambda c: c % 32)
    for n, part in enumerate(split(uat_ref[...])):
        kat_ref[n] = jnp.where(same, dot(dot(tall, part).astype(BF16), wide), 0.0).astype(BF16)
    copies = [
        pltpu.make_async_copy(ka_ref, ka_hbm, sems.at[0]),
        pltpu.make_async_copy(kat_ref, kat_hbm, sems.at[1]),
    ]
    for copy in copies:
        copy.start()
    for copy in copies:
        copy.wait()


def prep(u_a, u_at):
    return pl.pallas_call(
        prep_kernel,
        out_shape=(
            jax.ShapeDtypeStruct((2, 1024, 512), BF16),
            jax.ShapeDtypeStruct((2, 512, 1024), BF16),
        ),
        in_specs=[VMEM] * 2,
        out_specs=(HBM, HBM),
        scratch_shapes=[
            pltpu.VMEM((2, 1024, 512), BF16),
            pltpu.VMEM((2, 512, 1024), BF16),
            pltpu.SemaphoreType.DMA((2,)),
        ],
        compiler_params=pltpu.CompilerParams(vmem_limit_bytes=56 * 1024 * 1024),
        name="prep",
    )(u_a, u_at)


def mid_kernel(x_ref, pk_ref, ka_hbm, kat_hbm, old_hbm, w_hbm, core_ref, ka_ref, kat_ref, w_ref, sems):
    ka_copy = pltpu.make_async_copy(ka_hbm, ka_ref, sems.at[8])
    kat_copy = pltpu.make_async_copy(kat_hbm, kat_ref, sems.at[9])
    ka_copy.start()
    kat_copy.start()
    me = lax.axis_index("chan")

    def gathered(at, rows):
        parts = []
        for c in range(16):
            dz, dx = place(c, me)
            parts.append(pk_ref[dx, dz, at : at + rows, :])
        return jnp.concatenate(parts, axis=0)

    ui = gathered(64, 32)
    uit = split(ui.T)
    ui = split(ui)
    part = [dot3(uit, split(x_ref[:, m].reshape(512, 128))) for m in range(8)]
    part = split(jnp.concatenate(part, axis=1))
    ka_copy.wait()
    core = dot3(part, (ka_ref[0], ka_ref[1]))
    dirs = []
    for q in range(4):
        mine = core[:, q * 128 : q * 128 + 128]
        for c in range(16):
            dz, dx = place(me, c)
            core_ref[dz, dx, q * 8 : q * 8 + 8, :] = mine[c * 8 : c * 8 + 8]
        new_first, new_second = adam(mine, gathered(q * 8, 8), gathered(32 + q * 8, 8))
        dirs.append(
            new_first / (1.0 - beta_one**STEP) / (jnp.sqrt(new_second / (1.0 - beta_two**STEP)) + 1e-08)
        )
    kat_copy.wait()
    back = dot3(split(jnp.concatenate(dirs, axis=1)), (kat_ref[0], kat_ref[1]))
    copies = []
    for m in range(8):
        wide = dot3(ui, split(back[:, m * 128 : m * 128 + 128]))
        w_ref[:, m] = wide.reshape(16, 32, 128)
        copies.append(pltpu.make_async_copy(w_ref.at[:, m], w_hbm.at[:, m], sems.at[m]))
        copies[m].start()
    for copy in copies:
        copy.wait()


def mid(x, packed, ka, kat, old):
    return pl.pallas_call(
        mid_kernel,
        out_shape=(
            jax.ShapeDtypeStruct((16, 8, 32, 128), F32),
            jax.ShapeDtypeStruct((4, 4, 32, 128), F32),
        ),
        in_specs=[VMEM, VMEM, HBM, HBM, HBM],
        out_specs=(HBM, VMEM),
        scratch_shapes=[
            pltpu.VMEM((2, 1024, 512), BF16),
            pltpu.VMEM((2, 512, 1024), BF16),
            pltpu.VMEM((16, 8, 32, 128), F32),
            pltpu.SemaphoreType.DMA((10,)),
        ],
        compiler_params=pltpu.CompilerParams(vmem_limit_bytes=48 * 1024 * 1024),
        input_output_aliases={4: 0},
        name="mid",
    )(x, packed, ka, kat, old)


def moments_kernel(c_ref, fm_ref, sm_ref, nf_ref, ns_ref):
    me = lax.axis_index("chan")
    for p in range(2):
        at = [place(p * 8 + j, me) for j in range(8)]
        for q in range(4):
            tiles = swap_groups([c_ref[dx, dz, q * 8 : q * 8 + 8, :] for dz, dx in at])
            for x in range(8):
                s = q * 8 + x
                new_first, new_second = adam(tiles[x], fm_ref[:, p, s, :], sm_ref[:, p, s, :])
                nf_ref[:, p, s, :] = new_first
                ns_ref[:, p, s, :] = new_second


def moments(core, fm, sm):
    return pl.pallas_call(
        moments_kernel,
        out_shape=(jax.ShapeDtypeStruct(fm.shape, F32), jax.ShapeDtypeStruct(sm.shape, F32)),
        compiler_params=pltpu.CompilerParams(vmem_limit_bytes=VMEM_LIMIT),
        name="moments",
    )(core, fm, sm)


def tail_kernel(v_ref, w_ref, uo_ref, ubt_ref, o_ref, kb_ref):
    @pl.when(pl.program_id(0) == 0)
    def _():
        hi, lo = spread_b(ubt_ref[...])
        kb_ref[...] = jnp.concatenate([hi.T, hi.T, lo.T], axis=1)

    kb = kb_ref[...]
    uo = uo_ref[...]
    rows = pl.ds(pl.program_id(0) * 8, 8)
    for p in range(2):
        tiles = swap_groups([v_ref[p * 8 + j, :, rows, :].reshape(64, 128) for j in range(8)])
        for pair in range(2):
            wide = []
            for a in (2 * pair, 2 * pair + 1):
                both = [t.reshape(8, 8, 128) for t in tiles[2 * a : 2 * a + 2]]
                wide.append(jnp.stack(both, axis=1).reshape(128, 128))
            hi, lo = split(jnp.concatenate(wide, axis=1))
            expanded = dot(kb, jnp.concatenate([hi, lo, hi], axis=0)).astype(BF16)
            for n in range(2):
                a = 2 * pair + n
                update = dot(expanded[:, n * 128 : n * 128 + 128], uo, ((1,), (1,))).reshape(8, 32, 256)
                o_ref[:, p, a] = (w_ref[:, p, a].astype(F32) - step_rate * update).astype(BF16)


def tail(v, weight, u_out, ub_t):
    return pl.pallas_call(
        tail_kernel,
        grid=(4,),
        in_specs=[
            VMEM,
            pl.BlockSpec((8, 2, 4, 32, 256), lambda g: (g, 0, 0, 0, 0)),
            pl.BlockSpec((256, 128), lambda g: (0, 0)),
            pl.BlockSpec((16, 32), lambda g: (0, 0)),
        ],
        out_specs=pl.BlockSpec((8, 2, 4, 32, 256), lambda g: (g, 0, 0, 0, 0)),
        out_shape=jax.ShapeDtypeStruct((32, 2, 4, 32, 256), BF16),
        scratch_shapes=[pltpu.VMEM((256, 384), BF16)],
        compiler_params=pltpu.CompilerParams(vmem_limit_bytes=48 * 1024 * 1024),
        name="tail",
    )(v, weight, u_out, ub_t)


def shards(weight, gradient, first_moment, second_moment, u_in, u_out, u_modes_a, u_modes_b):
    both = ("chan", "mode")
    ub_t = u_modes_b.T
    fm = first_moment.reshape(8, 2, 32, 128)
    sm = second_moment.reshape(8, 2, 32, 128)
    sent = head(gradient, u_out, ub_t).reshape(128, 32, 128)
    got = lax.all_to_all(sent, both, 0, 0, tiled=True).reshape(16, 8, 32, 128)
    packed = exchange(pack(fm, sm, u_in, sent))
    ka, kat = prep(u_modes_a, u_modes_a.T)
    wide, core = mid(got, packed, ka, kat, sent.reshape(got.shape))
    wide = lax.all_to_all(wide.reshape(128, 32, 128), both, 0, 0, tiled=True)
    core = exchange(core)
    new_first, new_second = moments(core, fm, sm)
    new_weight = tail(wide.reshape(16, 8, 32, 128), weight, u_out, ub_t)
    return new_weight, new_first.reshape(first_moment.shape), new_second.reshape(second_moment.shape)


def solution(mesh):
    in_specs = (
        P("chan", None, "mode", None, None),
        P("chan", None, "mode", None, None),
        P("chan", None, None, "mode", None),
        P("chan", None, None, "mode", None),
        P("chan", None),
        P(),
        P(),
        P(),
    )
    out_specs = (
        P("chan", None, "mode", None, None),
        P("chan", None, None, "mode", None),
        P("chan", None, None, "mode", None),
    )
    return jax.shard_map(shards, mesh=mesh, in_specs=in_specs, out_specs=out_specs, check_vma=False)
```

```python
import jax
import jax.numpy as jnp
from jax import lax
from jax.experimental import pallas as pl
from jax.experimental.pallas import tpu as pltpu
from jax.sharding import PartitionSpec as P


STEP = 4
beta_one = 0.9
beta_two = 0.999
step_rate = 0.5

F32 = jnp.float32
BF16 = jnp.bfloat16
VMEM_LIMIT = 24 * 1024 * 1024
VMEM = pl.BlockSpec(memory_space=pltpu.VMEM)
HBM = pl.BlockSpec(memory_space=pltpu.HBM)


def dot(a, b, dims=((1,), (0,))):
    return lax.dot_general(a, b, (dims, ((), ())), preferred_element_type=F32)


def split(x):
    hi = x.astype(BF16)
    return hi, (x - hi.astype(F32)).astype(BF16)


def dot3(a, b, dims=((1,), (0,))):
    return dot(a[0], b[0], dims) + (dot(a[0], b[1], dims) + dot(a[1], b[0], dims))


def swap_groups(tiles):
    lane = lax.broadcasted_iota(jnp.int32, tiles[0].shape, tiles[0].ndim - 1)
    axis = tiles[0].ndim - 1
    for bit in (1, 2, 4):
        upper = (lane & (16 * bit)) != 0
        out = list(tiles)
        for x in range(8):
            if x & bit:
                continue
            low, high = tiles[x], tiles[x + bit]
            out[x] = jnp.where(upper, pltpu.roll(high, 16 * bit, axis), low)
            out[x + bit] = jnp.where(upper, high, pltpu.roll(low, 128 - 16 * bit, axis))
        tiles = out
    return tiles


def one_hot(shape, row_of, col_of):
    rows = lax.broadcasted_iota(jnp.int32, shape, 0)
    cols = lax.broadcasted_iota(jnp.int32, shape, 1)
    return row_of(rows) == col_of(cols)


def spread_b(ub_t):
    rows = one_hot((128, 16), lambda r: r // 8, lambda c: c).astype(BF16)
    cols = one_hot((32, 256), lambda r: r, lambda c: c % 32).astype(BF16)
    same = one_hot((128, 256), lambda r: r % 8, lambda c: c // 32)
    return [
        jnp.where(same, dot(dot(rows, part).astype(BF16), cols), 0.0).astype(BF16)
        for part in split(ub_t)
    ]


def head_kernel(g_ref, uo_ref, ubt_ref, z_ref, kb_ref):
    @pl.when(pl.program_id(0) == 0)
    def _():
        hi, lo = spread_b(ubt_ref[...])
        kb_ref[0:128, :] = hi
        kb_ref[128:256, :] = lo

    kb = kb_ref[...]
    uo = uo_ref[...]
    for p in range(2):
        tiles = []
        for a in range(4):
            both = dot(kb, g_ref[:, p, a].reshape(256, 256))
            hi, lo = split(both[0:128] + both[128:256])
            nar = (dot(hi, uo) + dot(lo, uo)).reshape(8, 2, 8, 128)
            tiles += [nar[:, 0].reshape(64, 128), nar[:, 1].reshape(64, 128)]
        tiles = swap_groups(tiles)
        for j in range(8):
            z_ref[p * 8 + j] = tiles[j].reshape(8, 8, 128)


def head(gradient, u_out, ub_t):
    return pl.pallas_call(
        head_kernel,
        grid=(4,),
        in_specs=[
            pl.BlockSpec((8, 2, 4, 32, 256), lambda g: (g, 0, 0, 0, 0)),
            pl.BlockSpec((256, 128), lambda g: (0, 0)),
            pl.BlockSpec((16, 32), lambda g: (0, 0)),
        ],
        out_specs=pl.BlockSpec((16, 8, 8, 128), lambda g: (0, 0, g, 0)),
        out_shape=jax.ShapeDtypeStruct((16, 8, 32, 128), F32),
        scratch_shapes=[pltpu.VMEM((256, 256), BF16)],
        compiler_params=pltpu.CompilerParams(vmem_limit_bytes=54 * 1024 * 1024),
        name="head",
    )(gradient, u_out, ub_t)


def pack_kernel(fm_ref, sm_ref, ui_ref, after_ref, o_ref):
    me = lax.axis_index("chan")
    for p in range(2):
        tiles = {}
        for which, ref in enumerate((fm_ref, sm_ref)):
            for q in range(4):
                tiles[which, q] = swap_groups([ref[:, p, q * 8 + x, :] for x in range(8)])
        for j in range(8):
            e, f = pair_steps(me, p * 8 + j)
            for which in range(2):
                for q in range(4):
                    at = which * 32 + q * 8
                    o_ref[e, f, at : at + 8, :] = tiles[which, q][j]
            o_ref[e, f, 64:96, :] = ui_ref[...]


def pack(fm, sm, u_in, after):
    return pl.pallas_call(
        pack_kernel,
        in_specs=[VMEM, VMEM, VMEM, HBM],
        out_specs=VMEM,
        out_shape=jax.ShapeDtypeStruct((2, 8, 96, 128), F32),
        compiler_params=pltpu.CompilerParams(vmem_limit_bytes=VMEM_LIMIT),
        name="pack",
    )(fm, sm, u_in, after)


def pair_steps(c, other):
    shift = (other // 4 + 4 - c // 4) % 4 * 2 + (other // 2 + c // 2) % 2
    return (other + c) % 2, shift


def pair_exchange(blocks):
    across = lax.ppermute(blocks[1], "chan", [(c, c ^ 1) for c in range(16)])
    both = jnp.stack([blocks[0], across], axis=1)
    got = [both[0]]
    for f in range(1, 8):
        ring = [(c, (c // 4 + f // 2) % 4 * 4 + (c % 4 + f % 2 * 2) % 4) for c in range(16)]
        got.append(lax.ppermute(both[f], "chan", ring))
    return got


def adam(core, fm, sm):
    new_first = beta_one * fm + (1.0 - beta_one) * core
    new_second = beta_two * sm + (1.0 - beta_two) * core * core
    return new_first, new_second


def prep_kernel(uat_ref, ka_hbm, kat_hbm, ka_ref, kat_ref, sems):
    tall = one_hot((1024, 32), lambda r: r // 32, lambda c: c).astype(BF16)
    wide = one_hot((16, 512), lambda r: r, lambda c: c // 32).astype(BF16)
    same = one_hot((1024, 512), lambda r: r % 32, lambda c: c % 32)
    for n, part in enumerate(split(uat_ref[...])):
        rows = dot(tall, part, ((1,), (1,))).astype(BF16)
        ka_ref[n] = jnp.where(same, dot(rows, wide), 0.0).astype(BF16)
    tall = one_hot((512, 16), lambda r: r // 32, lambda c: c).astype(BF16)
    wide = one_hot((32, 1024), lambda r: r, lambda c: c // 32).astype(BF16)
    same = one_hot((512, 1024), lambda r: r % 32, lambda c: c % 32)
    for n, part in enumerate(split(uat_ref[...])):
        rows = dot(tall, part).astype(BF16)
        kat_ref[n] = jnp.where(same, dot(rows, wide), 0.0).astype(BF16)
    copies = [
        pltpu.make_async_copy(ka_ref, ka_hbm, sems.at[0]),
        pltpu.make_async_copy(kat_ref, kat_hbm, sems.at[1]),
    ]
    for copy in copies:
        copy.start()
    for copy in copies:
        copy.wait()


def prep(u_at):
    return pl.pallas_call(
        prep_kernel,
        out_shape=(
            jax.ShapeDtypeStruct((2, 1024, 512), BF16),
            jax.ShapeDtypeStruct((2, 512, 1024), BF16),
        ),
        in_specs=[VMEM],
        out_specs=(HBM, HBM),
        scratch_shapes=[
            pltpu.VMEM((2, 1024, 512), BF16),
            pltpu.VMEM((2, 512, 1024), BF16),
            pltpu.SemaphoreType.DMA((2,)),
        ],
        compiler_params=pltpu.CompilerParams(vmem_limit_bytes=56 * 1024 * 1024),
        name="prep",
    )(u_at)


def collect_kernel(*refs):
    for f in range(8):
        refs[8][f] = refs[f][...]


def collect(parts):
    return pl.pallas_call(
        collect_kernel,
        out_shape=jax.ShapeDtypeStruct((8, 2, 96, 128), F32),
        in_specs=[VMEM] * 8,
        out_specs=VMEM,
        compiler_params=pltpu.CompilerParams(vmem_limit_bytes=24 * 1024 * 1024),
        name="collect",
    )(*parts)


def mid_kernel(
    x_ref, ka_hbm, kat_hbm, old_hbm, pk_ref, w_hbm, core_ref, ka_ref, kat_ref, w_ref, sems
):
    ka_copy = pltpu.make_async_copy(ka_hbm, ka_ref, sems.at[8])
    kat_copy = pltpu.make_async_copy(kat_hbm, kat_ref, sems.at[9])
    ka_copy.start()
    kat_copy.start()
    me = lax.axis_index("chan")

    def gathered(at, rows):
        parts = []
        for c in range(16):
            e, f = pair_steps(c, me)
            parts.append(pk_ref[f, e, at : at + rows, :])
        return jnp.concatenate(parts, axis=0)

    x = [split(x_ref[:, m].reshape(512, 128)) for m in range(8)]
    ui = gathered(64, 32)
    uit = split(ui.T)
    ui = split(ui)
    part = split(jnp.concatenate([dot3(uit, x[m]) for m in range(8)], axis=1))
    ka_copy.wait()
    core = dot3(part, (ka_ref[0], ka_ref[1]))
    dirs = []
    for q in range(4):
        mine = core[:, q * 128 : q * 128 + 128]
        for c in range(16):
            e, f = pair_steps(me, c)
            core_ref[e, f, q * 8 : q * 8 + 8, :] = mine[c * 8 : c * 8 + 8]
        new_first, new_second = adam(mine, gathered(q * 8, 8), gathered(32 + q * 8, 8))
        dirs.append(
            new_first / (1.0 - beta_one**STEP) / (jnp.sqrt(new_second / (1.0 - beta_two**STEP)) + 1e-08)
        )
    kat_copy.wait()
    back = dot3(split(jnp.concatenate(dirs, axis=1)), (kat_ref[0], kat_ref[1]))
    copies = []
    for m in range(8):
        wide = dot3(ui, split(back[:, m * 128 : m * 128 + 128]))
        w_ref[:, m] = wide.reshape(16, 32, 128)
        copies.append(pltpu.make_async_copy(w_ref.at[:, m], w_hbm.at[:, m], sems.at[m]))
        copies[m].start()
    for copy in copies:
        copy.wait()


def mid(x, packed, ka, kat, old):
    return pl.pallas_call(
        mid_kernel,
        out_shape=(
            jax.ShapeDtypeStruct((16, 8, 32, 128), F32),
            jax.ShapeDtypeStruct((2, 8, 32, 128), F32),
        ),
        in_specs=[VMEM, HBM, HBM, HBM, VMEM],
        out_specs=(HBM, VMEM),
        scratch_shapes=[
            pltpu.VMEM((2, 1024, 512), BF16),
            pltpu.VMEM((2, 512, 1024), BF16),
            pltpu.VMEM((16, 8, 32, 128), F32),
            pltpu.SemaphoreType.DMA((10,)),
        ],
        compiler_params=pltpu.CompilerParams(vmem_limit_bytes=48 * 1024 * 1024),
        input_output_aliases={3: 0},
        name="mid",
    )(x, ka, kat, old, packed)


def moments_kernel(fm_ref, sm_ref, *refs):
    core, (nf_ref, ns_ref, c_ref) = refs[:8], refs[8:]
    me = lax.axis_index("chan")
    for f in range(8):
        c_ref[:, f] = core[f][...]
    for p in range(2):
        at = [pair_steps(p * 8 + j, me) for j in range(8)]
        for q in range(4):
            tiles = swap_groups([c_ref[e, f, q * 8 : q * 8 + 8, :] for e, f in at])
            for x in range(8):
                s = q * 8 + x
                new_first, new_second = adam(tiles[x], fm_ref[:, p, s, :], sm_ref[:, p, s, :])
                nf_ref[:, p, s, :] = new_first
                ns_ref[:, p, s, :] = new_second


def moments(core, fm, sm):
    return pl.pallas_call(
        moments_kernel,
        out_shape=(jax.ShapeDtypeStruct(fm.shape, F32), jax.ShapeDtypeStruct(sm.shape, F32)),
        scratch_shapes=[pltpu.VMEM((2, 8, 32, 128), F32)],
        compiler_params=pltpu.CompilerParams(vmem_limit_bytes=VMEM_LIMIT),
        name="moments",
    )(fm, sm, *core)


def tail_kernel(v_ref, w_ref, uo_ref, ubt_ref, o_ref, kb_ref):
    @pl.when(pl.program_id(0) == 0)
    def _():
        hi, lo = spread_b(ubt_ref[...])
        kb_ref[...] = jnp.concatenate([hi.T, hi.T, lo.T], axis=1)

    kb = kb_ref[...]
    uo = uo_ref[...]
    rows = pl.ds(pl.program_id(0) * 8, 8)
    for p in range(2):
        tiles = swap_groups([v_ref[p * 8 + j, :, rows, :].reshape(64, 128) for j in range(8)])
        for pair in range(2):
            wide = []
            for a in (2 * pair, 2 * pair + 1):
                both = [t.reshape(8, 8, 128) for t in tiles[2 * a : 2 * a + 2]]
                wide.append(jnp.stack(both, axis=1).reshape(128, 128))
            hi, lo = split(jnp.concatenate(wide, axis=1))
            expanded = dot(kb, jnp.concatenate([hi, lo, hi], axis=0)).astype(BF16)
            for n in range(2):
                a = 2 * pair + n
                update = dot(expanded[:, n * 128 : n * 128 + 128], uo, ((1,), (1,))).reshape(8, 32, 256)
                o_ref[:, p, a] = (w_ref[:, p, a].astype(F32) - step_rate * update).astype(BF16)


def tail(v, weight, u_out, ub_t):
    return pl.pallas_call(
        tail_kernel,
        grid=(4,),
        in_specs=[
            VMEM,
            pl.BlockSpec((8, 2, 4, 32, 256), lambda g: (g, 0, 0, 0, 0)),
            pl.BlockSpec((256, 128), lambda g: (0, 0)),
            pl.BlockSpec((16, 32), lambda g: (0, 0)),
        ],
        out_specs=pl.BlockSpec((8, 2, 4, 32, 256), lambda g: (g, 0, 0, 0, 0)),
        out_shape=jax.ShapeDtypeStruct((32, 2, 4, 32, 256), BF16),
        scratch_shapes=[pltpu.VMEM((256, 384), BF16)],
        compiler_params=pltpu.CompilerParams(vmem_limit_bytes=48 * 1024 * 1024),
        name="tail",
    )(v, weight, u_out, ub_t)


def shards(weight, gradient, first_moment, second_moment, u_in, u_out, u_modes_a, u_modes_b):
    both = ("chan", "mode")
    ub_t = u_modes_b.T
    fm = first_moment.reshape(8, 2, 32, 128)
    sm = second_moment.reshape(8, 2, 32, 128)
    sent = head(gradient, u_out, ub_t).reshape(128, 32, 128)
    got = lax.all_to_all(sent, both, 0, 0, tiled=True).reshape(16, 8, 32, 128)
    packed = collect(pair_exchange(pack(fm, sm, u_in, sent)))
    ka, kat = prep(u_modes_a.T)
    wide, core = mid(got, packed, ka, kat, sent.reshape(got.shape))
    wide = lax.all_to_all(wide.reshape(128, 32, 128), both, 0, 0, tiled=True)
    core = pair_exchange(core)
    new_first, new_second = moments(core, fm, sm)
    new_weight = tail(wide.reshape(16, 8, 32, 128), weight, u_out, ub_t)
    return new_weight, new_first.reshape(first_moment.shape), new_second.reshape(second_moment.shape)


def solution(mesh):
    in_specs = (
        P("chan", None, "mode", None, None),
        P("chan", None, "mode", None, None),
        P("chan", None, None, "mode", None),
        P("chan", None, None, "mode", None),
        P("chan", None),
        P(),
        P(),
        P(),
    )
    out_specs = (
        P("chan", None, "mode", None, None),
        P("chan", None, None, "mode", None),
        P("chan", None, None, "mode", None),
    )
    return jax.shard_map(shards, mesh=mesh, in_specs=in_specs, out_specs=out_specs, check_vma=False)
```

```python
import jax
import jax.numpy as jnp
from jax import lax
from jax.experimental import pallas as pl
from jax.experimental.pallas import tpu as pltpu
from jax.sharding import PartitionSpec as P


STEP = 4
beta_one = 0.9
beta_two = 0.999
step_rate = 0.5

F32 = jnp.float32
BF16 = jnp.bfloat16
VMEM_LIMIT = 24 * 1024 * 1024
VMEM = pl.BlockSpec(memory_space=pltpu.VMEM)
HBM = pl.BlockSpec(memory_space=pltpu.HBM)


def dot(a, b, dims=((1,), (0,))):
    return lax.dot_general(a, b, (dims, ((), ())), preferred_element_type=F32)


def split(x):
    hi = x.astype(BF16)
    return hi, (x - hi.astype(F32)).astype(BF16)


def dot3(a, b, dims=((1,), (0,))):
    return dot(a[0], b[0], dims) + (dot(a[0], b[1], dims) + dot(a[1], b[0], dims))


def swap_groups(tiles):
    lane = lax.broadcasted_iota(jnp.int32, tiles[0].shape, tiles[0].ndim - 1)
    axis = tiles[0].ndim - 1
    for bit in (1, 2, 4):
        upper = (lane & (16 * bit)) != 0
        out = list(tiles)
        for x in range(8):
            if x & bit:
                continue
            low, high = tiles[x], tiles[x + bit]
            out[x] = jnp.where(upper, pltpu.roll(high, 16 * bit, axis), low)
            out[x + bit] = jnp.where(upper, high, pltpu.roll(low, 128 - 16 * bit, axis))
        tiles = out
    return tiles


def one_hot(shape, row_of, col_of):
    rows = lax.broadcasted_iota(jnp.int32, shape, 0)
    cols = lax.broadcasted_iota(jnp.int32, shape, 1)
    return row_of(rows) == col_of(cols)


def spread_b(ub_t):
    rows = one_hot((128, 16), lambda r: r // 8, lambda c: c).astype(BF16)
    cols = one_hot((32, 256), lambda r: r, lambda c: c % 32).astype(BF16)
    same = one_hot((128, 256), lambda r: r % 8, lambda c: c // 32)
    return [
        jnp.where(same, dot(dot(rows, part).astype(BF16), cols), 0.0).astype(BF16)
        for part in split(ub_t)
    ]


def head_kernel(g_ref, uo_ref, ubt_ref, z_ref, kb_ref):
    @pl.when(pl.program_id(0) == 0)
    def _():
        hi, lo = spread_b(ubt_ref[...])
        kb_ref[0:128, :] = hi
        kb_ref[128:256, :] = lo

    kb = kb_ref[...]
    uo = uo_ref[...]
    for n, p in [(n, p) for n in range(2) for p in range(2)]:
        tiles = []
        for a in range(4):
            both = dot(kb, g_ref[n * 8 : n * 8 + 8, p, a].reshape(256, 256))
            hi, lo = split(both[0:128] + both[128:256])
            nar = (dot(hi, uo) + dot(lo, uo)).reshape(8, 2, 8, 128)
            tiles += [nar[:, 0].reshape(64, 128), nar[:, 1].reshape(64, 128)]
        tiles = swap_groups(tiles)
        for j in range(8):
            z_ref[p * 8 + j, :, n * 8 : n * 8 + 8, :] = tiles[j].reshape(8, 8, 128)


def head(gradient, u_out, ub_t):
    return pl.pallas_call(
        head_kernel,
        grid=(2,),
        in_specs=[
            pl.BlockSpec((16, 2, 4, 32, 256), lambda g: (g, 0, 0, 0, 0)),
            pl.BlockSpec((256, 128), lambda g: (0, 0)),
            pl.BlockSpec((16, 32), lambda g: (0, 0)),
        ],
        out_specs=pl.BlockSpec((16, 8, 16, 128), lambda g: (0, 0, g, 0)),
        out_shape=jax.ShapeDtypeStruct((16, 8, 32, 128), F32),
        scratch_shapes=[pltpu.VMEM((256, 256), BF16)],
        compiler_params=pltpu.CompilerParams(vmem_limit_bytes=54 * 1024 * 1024),
        name="head",
    )(gradient, u_out, ub_t)


def pack_kernel(fm_ref, sm_ref, ui_ref, after_ref, o_ref):
    me = lax.axis_index("chan")
    for p in range(2):
        tiles = {}
        for which, ref in enumerate((fm_ref, sm_ref)):
            for q in range(4):
                tiles[which, q] = swap_groups([ref[:, p, q * 8 + x, :] for x in range(8)])
        for j in range(8):
            e, f = pair_steps(me, p * 8 + j)
            for which in range(2):
                for q in range(4):
                    at = which * 32 + q * 8
                    o_ref[e, f, at : at + 8, :] = tiles[which, q][j]
            o_ref[e, f, 64:96, :] = ui_ref[...]


def pack(fm, sm, u_in, after):
    return pl.pallas_call(
        pack_kernel,
        in_specs=[VMEM, VMEM, VMEM, HBM],
        out_specs=VMEM,
        out_shape=jax.ShapeDtypeStruct((2, 8, 96, 128), F32),
        compiler_params=pltpu.CompilerParams(vmem_limit_bytes=VMEM_LIMIT),
        name="pack",
    )(fm, sm, u_in, after)


def pair_steps(c, other):
    shift = (other // 4 + 4 - c // 4) % 4 * 2 + (other // 2 + c // 2) % 2
    return (other + c) % 2, shift


def pair_exchange(blocks):
    across = lax.ppermute(blocks[1], "chan", [(c, c ^ 1) for c in range(16)])
    both = jnp.stack([blocks[0], across], axis=1)
    got = [both[0]]
    for f in range(1, 8):
        ring = [(c, (c // 4 + f // 2) % 4 * 4 + (c % 4 + f % 2 * 2) % 4) for c in range(16)]
        got.append(lax.ppermute(both[f], "chan", ring))
    return got


def adam(core, fm, sm):
    new_first = beta_one * fm + (1.0 - beta_one) * core
    new_second = beta_two * sm + (1.0 - beta_two) * core * core
    return new_first, new_second


def prep_kernel(uat_ref, ubt_ref, ka_hbm, kat_hbm, kb_hbm, ka_ref, kat_ref, kb_ref, sems):
    hi, lo = spread_b(ubt_ref[...])
    kb_ref[...] = jnp.concatenate([hi.T, hi.T, lo.T], axis=1)
    tall = one_hot((1024, 32), lambda r: r // 32, lambda c: c).astype(BF16)
    wide = one_hot((16, 512), lambda r: r, lambda c: c // 32).astype(BF16)
    same = one_hot((1024, 512), lambda r: r % 32, lambda c: c % 32)
    for n, part in enumerate(split(uat_ref[...])):
        rows = dot(tall, part, ((1,), (1,))).astype(BF16)
        ka_ref[n] = jnp.where(same, dot(rows, wide), 0.0).astype(BF16)
    tall = one_hot((512, 16), lambda r: r // 32, lambda c: c).astype(BF16)
    wide = one_hot((32, 1024), lambda r: r, lambda c: c // 32).astype(BF16)
    same = one_hot((512, 1024), lambda r: r % 32, lambda c: c % 32)
    for n, part in enumerate(split(uat_ref[...])):
        rows = dot(tall, part).astype(BF16)
        kat_ref[n] = jnp.where(same, dot(rows, wide), 0.0).astype(BF16)
    copies = [
        pltpu.make_async_copy(ka_ref, ka_hbm, sems.at[0]),
        pltpu.make_async_copy(kat_ref, kat_hbm, sems.at[1]),
        pltpu.make_async_copy(kb_ref, kb_hbm, sems.at[2]),
    ]
    for copy in copies:
        copy.start()
    for copy in copies:
        copy.wait()


def prep(u_at, ub_t):
    return pl.pallas_call(
        prep_kernel,
        out_shape=(
            jax.ShapeDtypeStruct((2, 1024, 512), BF16),
            jax.ShapeDtypeStruct((2, 512, 1024), BF16),
            jax.ShapeDtypeStruct((256, 384), BF16),
        ),
        in_specs=[VMEM] * 2,
        out_specs=(HBM,) * 3,
        scratch_shapes=[
            pltpu.VMEM((2, 1024, 512), BF16),
            pltpu.VMEM((2, 512, 1024), BF16),
            pltpu.VMEM((256, 384), BF16),
            pltpu.SemaphoreType.DMA((3,)),
        ],
        compiler_params=pltpu.CompilerParams(vmem_limit_bytes=56 * 1024 * 1024),
        name="prep",
    )(u_at, ub_t)


def collect_kernel(*refs):
    for f in range(8):
        refs[8][f] = refs[f][...]


def collect(parts):
    return pl.pallas_call(
        collect_kernel,
        out_shape=jax.ShapeDtypeStruct((8, 2, 96, 128), F32),
        in_specs=[VMEM] * 8,
        out_specs=VMEM,
        compiler_params=pltpu.CompilerParams(vmem_limit_bytes=24 * 1024 * 1024),
        name="collect",
    )(*parts)


def mid_kernel(
    x_ref, ka_hbm, kat_hbm, old_hbm, pk_ref, w_hbm, core_ref, ka_ref, kat_ref, w_ref, sems
):
    ka_copy = pltpu.make_async_copy(ka_hbm, ka_ref, sems.at[8])
    kat_copy = pltpu.make_async_copy(kat_hbm, kat_ref, sems.at[9])
    ka_copy.start()
    kat_copy.start()
    me = lax.axis_index("chan")

    def gathered(at, rows):
        parts = []
        for c in range(16):
            e, f = pair_steps(c, me)
            parts.append(pk_ref[f, e, at : at + rows, :])
        return jnp.concatenate(parts, axis=0)

    x = [split(x_ref[:, m].reshape(512, 128)) for m in range(8)]
    ui = gathered(64, 32)
    uit = split(ui.T)
    ui = split(ui)
    part = split(jnp.concatenate([dot3(uit, x[m]) for m in range(8)], axis=1))
    ka_copy.wait()
    core = dot3(part, (ka_ref[0], ka_ref[1]))
    dirs = []
    for q in range(4):
        mine = core[:, q * 128 : q * 128 + 128]
        for c in range(16):
            e, f = pair_steps(me, c)
            core_ref[e, f, q * 8 : q * 8 + 8, :] = mine[c * 8 : c * 8 + 8]
        new_first, new_second = adam(mine, gathered(q * 8, 8), gathered(32 + q * 8, 8))
        dirs.append(
            new_first / (1.0 - beta_one**STEP) / (jnp.sqrt(new_second / (1.0 - beta_two**STEP)) + 1e-08)
        )
    kat_copy.wait()
    back = dot3(split(jnp.concatenate(dirs, axis=1)), (kat_ref[0], kat_ref[1]))
    copies = []
    for m in range(8):
        wide = dot3(ui, split(back[:, m * 128 : m * 128 + 128]))
        w_ref[:, m] = wide.reshape(16, 32, 128)
        copies.append(pltpu.make_async_copy(w_ref.at[:, m], w_hbm.at[:, m], sems.at[m]))
        copies[m].start()
    for copy in copies:
        copy.wait()


def mid(x, packed, ka, kat, old):
    return pl.pallas_call(
        mid_kernel,
        out_shape=(
            jax.ShapeDtypeStruct((16, 8, 32, 128), F32),
            jax.ShapeDtypeStruct((2, 8, 32, 128), F32),
        ),
        in_specs=[VMEM, HBM, HBM, HBM, VMEM],
        out_specs=(HBM, VMEM),
        scratch_shapes=[
            pltpu.VMEM((2, 1024, 512), BF16),
            pltpu.VMEM((2, 512, 1024), BF16),
            pltpu.VMEM((16, 8, 32, 128), F32),
            pltpu.SemaphoreType.DMA((10,)),
        ],
        compiler_params=pltpu.CompilerParams(vmem_limit_bytes=48 * 1024 * 1024),
        input_output_aliases={3: 0},
        name="mid",
    )(x, ka, kat, old, packed)


def moments_kernel(fm_ref, sm_ref, *refs):
    core, (nf_ref, ns_ref, c_ref) = refs[:8], refs[8:]
    me = lax.axis_index("chan")
    for f in range(8):
        c_ref[:, f] = core[f][...]
    for p in range(2):
        at = [pair_steps(p * 8 + j, me) for j in range(8)]
        for q in range(4):
            tiles = swap_groups([c_ref[e, f, q * 8 : q * 8 + 8, :] for e, f in at])
            for x in range(8):
                s = q * 8 + x
                new_first, new_second = adam(tiles[x], fm_ref[:, p, s, :], sm_ref[:, p, s, :])
                nf_ref[:, p, s, :] = new_first
                ns_ref[:, p, s, :] = new_second


def moments(core, fm, sm):
    return pl.pallas_call(
        moments_kernel,
        out_shape=(jax.ShapeDtypeStruct(fm.shape, F32), jax.ShapeDtypeStruct(sm.shape, F32)),
        scratch_shapes=[pltpu.VMEM((2, 8, 32, 128), F32)],
        compiler_params=pltpu.CompilerParams(vmem_limit_bytes=VMEM_LIMIT),
        name="moments",
    )(fm, sm, *core)


def tail_kernel(v_ref, w_ref, uo_ref, kb_ref, o_ref):
    kb = kb_ref[...]
    uo = uo_ref[...]
    for k, p in [(k, p) for k in range(2) for p in range(2)]:
        rows = pl.ds(pl.program_id(0) * 16 + k * 8, 8)
        mine = slice(k * 8, k * 8 + 8)
        tiles = swap_groups([v_ref[p * 8 + j, :, rows, :].reshape(64, 128) for j in range(8)])
        for pair in range(2):
            wide = []
            for a in (2 * pair, 2 * pair + 1):
                both = [t.reshape(8, 8, 128) for t in tiles[2 * a : 2 * a + 2]]
                wide.append(jnp.stack(both, axis=1).reshape(128, 128))
            hi, lo = split(jnp.concatenate(wide, axis=1))
            expanded = dot(kb, jnp.concatenate([hi, lo, hi], axis=0)).astype(BF16)
            for n in range(2):
                a = 2 * pair + n
                update = dot(expanded[:, n * 128 : n * 128 + 128], uo, ((1,), (1,))).reshape(8, 32, 256)
                o_ref[mine, p, a] = (w_ref[mine, p, a].astype(F32) - step_rate * update).astype(BF16)


def tail(v, weight, u_out, kb):
    return pl.pallas_call(
        tail_kernel,
        grid=(2,),
        in_specs=[
            VMEM,
            pl.BlockSpec((16, 2, 4, 32, 256), lambda g: (g, 0, 0, 0, 0)),
            pl.BlockSpec((256, 128), lambda g: (0, 0)),
            pl.BlockSpec((256, 384), lambda g: (0, 0)),
        ],
        out_specs=pl.BlockSpec((16, 2, 4, 32, 256), lambda g: (g, 0, 0, 0, 0)),
        out_shape=jax.ShapeDtypeStruct((32, 2, 4, 32, 256), BF16),
        compiler_params=pltpu.CompilerParams(vmem_limit_bytes=48 * 1024 * 1024),
        name="tail",
    )(v, weight, u_out, kb)


def shards(weight, gradient, first_moment, second_moment, u_in, u_out, u_modes_a, u_modes_b):
    both = ("chan", "mode")
    ub_t = u_modes_b.T
    fm = first_moment.reshape(8, 2, 32, 128)
    sm = second_moment.reshape(8, 2, 32, 128)
    sent = head(gradient, u_out, ub_t).reshape(128, 32, 128)
    got = lax.all_to_all(sent, both, 0, 0, tiled=True).reshape(16, 8, 32, 128)
    packed = collect(pair_exchange(pack(fm, sm, u_in, sent)))
    ka, kat, kb = prep(u_modes_a.T, ub_t)
    wide, core = mid(got, packed, ka, kat, sent.reshape(got.shape))
    wide = lax.all_to_all(wide.reshape(128, 32, 128), both, 0, 0, tiled=True)
    core = pair_exchange(core)
    new_first, new_second = moments(core, fm, sm)
    new_weight = tail(wide.reshape(16, 8, 32, 128), weight, u_out, kb)
    return new_weight, new_first.reshape(first_moment.shape), new_second.reshape(second_moment.shape)


def solution(mesh):
    in_specs = (
        P("chan", None, "mode", None, None),
        P("chan", None, "mode", None, None),
        P("chan", None, None, "mode", None),
        P("chan", None, None, "mode", None),
        P("chan", None),
        P(),
        P(),
        P(),
    )
    out_specs = (
        P("chan", None, "mode", None, None),
        P("chan", None, None, "mode", None),
        P("chan", None, None, "mode", None),
    )
    return jax.shard_map(shards, mesh=mesh, in_specs=in_specs, out_specs=out_specs, check_vma=False)
```

```python
import jax
import jax.numpy as jnp
from jax import lax
from jax.experimental import pallas as pl
from jax.experimental.pallas import tpu as pltpu
from jax.sharding import PartitionSpec as P


STEP = 4
beta_one = 0.9
beta_two = 0.999
step_rate = 0.5

F32 = jnp.float32
BF16 = jnp.bfloat16
VMEM_LIMIT = 24 * 1024 * 1024
VMEM = pl.BlockSpec(memory_space=pltpu.VMEM)
HBM = pl.BlockSpec(memory_space=pltpu.HBM)


def dot(a, b, dims=((1,), (0,))):
    return lax.dot_general(a, b, (dims, ((), ())), preferred_element_type=F32)


def split(x):
    hi = x.astype(BF16)
    return hi, (x - hi.astype(F32)).astype(BF16)


def stack(x):
    hi, lo = split(x)
    return jnp.concatenate([hi, lo], axis=0), hi


def dot3(a, b):
    both = dot(a[0], b[0])
    rows = both.shape[0] // 2
    return both[:rows] + (both[rows:] + dot(a[1], b[1]))


def swap_groups(tiles):
    axis = tiles[0].ndim - 1
    lane = lax.broadcasted_iota(jnp.int32, tiles[0].shape, axis)
    skewed = [tiles[0]] + [pltpu.roll(tiles[x], 16 * x, axis) for x in range(1, 8)]
    out = [skewed[-y % 8] for y in range(8)]
    for bit in (1, 2, 4):
        pick = (lane & (16 * bit)) != 0
        out = [jnp.where(pick, out[(y - bit) % 8], out[y]) for y in range(8)]
    return [out[0]] + [pltpu.roll(out[y], 128 - 16 * y, axis) for y in range(1, 8)]


def one_hot(shape, row_of, col_of):
    rows = lax.broadcasted_iota(jnp.int32, shape, 0)
    cols = lax.broadcasted_iota(jnp.int32, shape, 1)
    return row_of(rows) == col_of(cols)


def spread_b(ub_t):
    rows = one_hot((128, 16), lambda r: r // 8, lambda c: c).astype(BF16)
    cols = one_hot((32, 256), lambda r: r, lambda c: c % 32).astype(BF16)
    same = one_hot((128, 256), lambda r: r % 8, lambda c: c // 32)
    return [
        jnp.where(same, dot(dot(rows, part).astype(BF16), cols), 0.0).astype(BF16)
        for part in split(ub_t)
    ]


def head_kernel(g_ref, uo_ref, ubt_ref, z_ref, kb_ref):
    @pl.when(pl.program_id(0) == 0)
    def _():
        hi, lo = spread_b(ubt_ref[...])
        kb_ref[0:128, :] = hi
        kb_ref[128:256, :] = lo

    kb = kb_ref[...]
    uo = uo_ref[...]
    for n, p in [(n, p) for n in range(2) for p in range(2)]:
        tiles = []
        for a in range(4):
            both = dot(kb, g_ref[n * 8 : n * 8 + 8, p, a].reshape(256, 256))
            both = dot(stack(both[0:128] + both[128:256])[0], uo)
            nar = (both[0:128] + both[128:256]).reshape(8, 2, 8, 128)
            tiles += [nar[:, 0].reshape(64, 128), nar[:, 1].reshape(64, 128)]
        tiles = swap_groups(tiles)
        for j in range(8):
            z_ref[p * 8 + j, :, n * 8 : n * 8 + 8, :] = tiles[j].reshape(8, 8, 128)


def head(gradient, u_out, ub_t):
    return pl.pallas_call(
        head_kernel,
        grid=(2,),
        in_specs=[
            pl.BlockSpec((16, 2, 4, 32, 256), lambda g: (g, 0, 0, 0, 0)),
            pl.BlockSpec((256, 128), lambda g: (0, 0)),
            pl.BlockSpec((16, 32), lambda g: (0, 0)),
        ],
        out_specs=pl.BlockSpec((16, 8, 16, 128), lambda g: (0, 0, g, 0)),
        out_shape=jax.ShapeDtypeStruct((16, 8, 32, 128), F32),
        scratch_shapes=[pltpu.VMEM((256, 256), BF16)],
        compiler_params=pltpu.CompilerParams(vmem_limit_bytes=54 * 1024 * 1024),
        name="head",
    )(gradient, u_out, ub_t)


def shift_steps(c, other):
    return (other // 4 + 4 - c // 4) % 4 * 2 + (other // 2 + c // 2) % 2


def by_parity(me, even, odd):
    own = me % 2 == 0
    return jnp.where(own, even, odd), jnp.where(own, odd, even)


def pair_exchange(own, cross):
    across = lax.ppermute(cross, "chan", [(c, c ^ 1) for c in range(16)])
    both = jnp.stack([own, across], axis=1)
    got = [both[0]]
    for f in range(1, 8):
        ring = [(c, (c // 4 + f // 2) % 4 * 4 + (c % 4 + f % 2 * 2) % 4) for c in range(16)]
        got.append(lax.ppermute(both[f], "chan", ring))
    return got


def pack_kernel(fm_ref, sm_ref, ui_ref, after_ref, own_ref, cross_ref):
    me = lax.axis_index("chan")
    for p in range(2):
        tiles = {}
        for which, ref in enumerate((fm_ref, sm_ref)):
            for q in range(4):
                tiles[which, q] = swap_groups([ref[:, p, q * 8 + x, :] for x in range(8)])
        for j in range(0, 8, 2):
            f = shift_steps(me, p * 8 + j)
            for which in range(2):
                for q in range(4):
                    at = slice(which * 32 + q * 8, which * 32 + q * 8 + 8)
                    pair = by_parity(me, tiles[which, q][j], tiles[which, q][j + 1])
                    own_ref[f, at, :], cross_ref[f, at, :] = pair
            own_ref[f, 64:96, :] = ui_ref[...]
            cross_ref[f, 64:96, :] = ui_ref[...]


def pack(fm, sm, u_in, after):
    return pl.pallas_call(
        pack_kernel,
        in_specs=[VMEM, VMEM, VMEM, HBM],
        out_specs=(VMEM, VMEM),
        out_shape=(jax.ShapeDtypeStruct((8, 96, 128), F32),) * 2,
        compiler_params=pltpu.CompilerParams(vmem_limit_bytes=VMEM_LIMIT),
        name="pack",
    )(fm, sm, u_in, after)


def adam(core, fm, sm):
    new_first = beta_one * fm + (1.0 - beta_one) * core
    new_second = beta_two * sm + (1.0 - beta_two) * core * core
    return new_first, new_second


def prep_kernel(uat_ref, ubt_ref, ka_hbm, kat_hbm, kb_hbm, ka_ref, kat_ref, kb_ref, sems):
    hi, lo = spread_b(ubt_ref[...])
    kb_ref[...] = jnp.concatenate([hi.T, hi.T, lo.T], axis=1)
    tall = one_hot((1024, 32), lambda r: r // 32, lambda c: c).astype(BF16)
    wide = one_hot((16, 512), lambda r: r, lambda c: c // 32).astype(BF16)
    same = one_hot((1024, 512), lambda r: r % 32, lambda c: c % 32)
    for n, part in enumerate(split(uat_ref[...])):
        rows = dot(tall, part, ((1,), (1,))).astype(BF16)
        ka_ref[n] = jnp.where(same, dot(rows, wide), 0.0).astype(BF16)
    tall = one_hot((512, 16), lambda r: r // 32, lambda c: c).astype(BF16)
    wide = one_hot((32, 1024), lambda r: r, lambda c: c // 32).astype(BF16)
    same = one_hot((512, 1024), lambda r: r % 32, lambda c: c % 32)
    for n, part in enumerate(split(uat_ref[...])):
        rows = dot(tall, part).astype(BF16)
        kat_ref[n] = jnp.where(same, dot(rows, wide), 0.0).astype(BF16)
    copies = [
        pltpu.make_async_copy(ka_ref, ka_hbm, sems.at[0]),
        pltpu.make_async_copy(kat_ref, kat_hbm, sems.at[1]),
        pltpu.make_async_copy(kb_ref, kb_hbm, sems.at[2]),
    ]
    for copy in copies:
        copy.start()
    for copy in copies:
        copy.wait()


def prep(u_at, ub_t):
    return pl.pallas_call(
        prep_kernel,
        out_shape=(
            jax.ShapeDtypeStruct((2, 1024, 512), BF16),
            jax.ShapeDtypeStruct((2, 512, 1024), BF16),
            jax.ShapeDtypeStruct((256, 384), BF16),
        ),
        in_specs=[VMEM] * 2,
        out_specs=(HBM,) * 3,
        scratch_shapes=[
            pltpu.VMEM((2, 1024, 512), BF16),
            pltpu.VMEM((2, 512, 1024), BF16),
            pltpu.VMEM((256, 384), BF16),
            pltpu.SemaphoreType.DMA((3,)),
        ],
        compiler_params=pltpu.CompilerParams(vmem_limit_bytes=56 * 1024 * 1024),
        name="prep",
    )(u_at, ub_t)


def collect_kernel(*refs):
    for f in range(8):
        refs[8][f] = refs[f][...]


def collect(parts):
    return pl.pallas_call(
        collect_kernel,
        out_shape=jax.ShapeDtypeStruct((8, 2, 96, 128), F32),
        in_specs=[VMEM] * 8,
        out_specs=VMEM,
        compiler_params=pltpu.CompilerParams(vmem_limit_bytes=24 * 1024 * 1024),
        name="collect",
    )(*parts)


def mid_kernel(
    x_ref, ka_hbm, kat_hbm, old_hbm, pk_ref, w_hbm, own_hbm, cross_hbm,
    ka_ref, kat_ref, w_ref, own_ref, cross_ref, sems,
):
    ka_copy = pltpu.make_async_copy(ka_hbm, ka_ref, sems.at[8])
    kat_copy = pltpu.make_async_copy(kat_hbm, kat_ref, sems.at[9])
    ka_copy.start()
    kat_copy.start()
    me = lax.axis_index("chan")

    def gathered(at, rows):
        parts = []
        for c in range(16):
            parts.append(pk_ref[shift_steps(c, me), (c + me) % 2, at : at + rows, :])
        return jnp.concatenate(parts, axis=0)

    ui = gathered(64, 32)
    uit = stack(ui.T)
    part = []
    for m in range(0, 8, 2):
        x = [x_ref[:, m].reshape(512, 128), x_ref[:, m + 1].reshape(512, 128)]
        part.append(dot3(uit, split(jnp.concatenate(x, axis=1))))
    part = stack(jnp.concatenate(part, axis=1))
    ka_copy.wait()
    core = dot3(part, (ka_ref[0], ka_ref[1]))
    dirs = []
    for q in range(4):
        mine = core[:, q * 128 : q * 128 + 128]
        at = slice(q * 8, q * 8 + 8)
        for c in range(0, 16, 2):
            f = shift_steps(me, c)
            pair = by_parity(me, mine[c * 8 : c * 8 + 8], mine[c * 8 + 8 : c * 8 + 16])
            own_ref[f, at, :], cross_ref[f, at, :] = pair
        new_first, new_second = adam(mine, gathered(q * 8, 8), gathered(32 + q * 8, 8))
        dirs.append(
            new_first / (1.0 - beta_one**STEP) / (jnp.sqrt(new_second / (1.0 - beta_two**STEP)) + 1e-08)
        )
    copies = [
        pltpu.make_async_copy(own_ref, own_hbm, sems.at[10]),
        pltpu.make_async_copy(cross_ref, cross_hbm, sems.at[11]),
    ]
    for copy in copies:
        copy.start()
    kat_copy.wait()
    back = dot3(stack(jnp.concatenate(dirs, axis=1)), (kat_ref[0], kat_ref[1]))
    ui = stack(ui)
    for n in range(4):
        wide = dot3(ui, split(back[:, n * 256 : n * 256 + 256]))
        for m in range(2):
            at = 2 * n + m
            w_ref[:, at] = wide[:, m * 128 : m * 128 + 128].reshape(16, 32, 128)
            copies.append(pltpu.make_async_copy(w_ref.at[:, at], w_hbm.at[:, at], sems.at[at]))
            copies[-1].start()
    for copy in copies:
        copy.wait()


def mid(x, packed, ka, kat, old):
    return pl.pallas_call(
        mid_kernel,
        out_shape=(
            jax.ShapeDtypeStruct((16, 8, 32, 128), F32),
            jax.ShapeDtypeStruct((8, 32, 128), F32),
            jax.ShapeDtypeStruct((8, 32, 128), F32),
        ),
        in_specs=[VMEM, HBM, HBM, HBM, VMEM],
        out_specs=(HBM,) * 3,
        scratch_shapes=[
            pltpu.VMEM((2, 1024, 512), BF16),
            pltpu.VMEM((2, 512, 1024), BF16),
            pltpu.VMEM((16, 8, 32, 128), F32),
            pltpu.VMEM((8, 32, 128), F32),
            pltpu.VMEM((8, 32, 128), F32),
            pltpu.SemaphoreType.DMA((12,)),
        ],
        compiler_params=pltpu.CompilerParams(vmem_limit_bytes=48 * 1024 * 1024),
        input_output_aliases={3: 0},
        name="mid",
    )(x, ka, kat, old, packed)


def moments_kernel(fm_ref, sm_ref, *refs):
    core, (nf_ref, ns_ref, c_ref) = refs[:8], refs[8:]
    me = lax.axis_index("chan")
    for f in range(8):
        c_ref[:, f] = core[f][...]
    for p in range(2):
        at = [((j + me) % 2, shift_steps(p * 8 + j, me)) for j in range(8)]
        for q in range(4):
            tiles = swap_groups([c_ref[e, f, q * 8 : q * 8 + 8, :] for e, f in at])
            for x in range(8):
                s = q * 8 + x
                new_first, new_second = adam(tiles[x], fm_ref[:, p, s, :], sm_ref[:, p, s, :])
                nf_ref[:, p, s, :] = new_first
                ns_ref[:, p, s, :] = new_second


def moments(core, fm, sm):
    return pl.pallas_call(
        moments_kernel,
        out_shape=(jax.ShapeDtypeStruct(fm.shape, F32), jax.ShapeDtypeStruct(sm.shape, F32)),
        scratch_shapes=[pltpu.VMEM((2, 8, 32, 128), F32)],
        compiler_params=pltpu.CompilerParams(vmem_limit_bytes=VMEM_LIMIT),
        name="moments",
    )(fm, sm, *core)


def tail_kernel(v_ref, w_ref, uo_ref, kb_ref, o_ref):
    kb = kb_ref[...]
    uo = uo_ref[...]
    for k, p in [(k, p) for k in range(2) for p in range(2)]:
        rows = pl.ds(pl.program_id(0) * 16 + k * 8, 8)
        mine = slice(k * 8, k * 8 + 8)
        tiles = swap_groups([v_ref[p * 8 + j, :, rows, :].reshape(64, 128) for j in range(8)])
        for pair in range(2):
            wide = []
            for a in (2 * pair, 2 * pair + 1):
                both = [t.reshape(8, 8, 128) for t in tiles[2 * a : 2 * a + 2]]
                wide.append(jnp.stack(both, axis=1).reshape(128, 128))
            hi, lo = split(jnp.concatenate(wide, axis=1))
            expanded = dot(kb, jnp.concatenate([hi, lo, hi], axis=0)).astype(BF16)
            expanded = jnp.concatenate([expanded[:, :128], expanded[:, 128:]], axis=0)
            update = dot(expanded, uo, ((1,), (1,))).reshape(2, 8, 32, 256)
            for n in range(2):
                a = 2 * pair + n
                o_ref[mine, p, a] = (w_ref[mine, p, a].astype(F32) - step_rate * update[n]).astype(BF16)


def tail(v, weight, u_out, kb):
    return pl.pallas_call(
        tail_kernel,
        grid=(2,),
        in_specs=[
            VMEM,
            pl.BlockSpec((16, 2, 4, 32, 256), lambda g: (g, 0, 0, 0, 0)),
            pl.BlockSpec((256, 128), lambda g: (0, 0)),
            pl.BlockSpec((256, 384), lambda g: (0, 0)),
        ],
        out_specs=pl.BlockSpec((16, 2, 4, 32, 256), lambda g: (g, 0, 0, 0, 0)),
        out_shape=jax.ShapeDtypeStruct((32, 2, 4, 32, 256), BF16),
        compiler_params=pltpu.CompilerParams(vmem_limit_bytes=48 * 1024 * 1024),
        name="tail",
    )(v, weight, u_out, kb)


def shards(weight, gradient, first_moment, second_moment, u_in, u_out, u_modes_a, u_modes_b):
    both = ("chan", "mode")
    ub_t = u_modes_b.T
    fm = first_moment.reshape(8, 2, 32, 128)
    sm = second_moment.reshape(8, 2, 32, 128)
    sent = head(gradient, u_out, ub_t).reshape(128, 32, 128)
    got = lax.all_to_all(sent, both, 0, 0, tiled=True).reshape(16, 8, 32, 128)
    packed = collect(pair_exchange(*pack(fm, sm, u_in, sent)))
    ka, kat, kb = prep(u_modes_a.T, ub_t)
    wide, own, cross = mid(got, packed, ka, kat, sent.reshape(got.shape))
    wide = lax.all_to_all(wide.reshape(128, 32, 128), both, 0, 0, tiled=True)
    core = pair_exchange(own, cross)
    new_first, new_second = moments(core, fm, sm)
    new_weight = tail(wide.reshape(16, 8, 32, 128), weight, u_out, kb)
    return new_weight, new_first.reshape(first_moment.shape), new_second.reshape(second_moment.shape)


def solution(mesh):
    in_specs = (
        P("chan", None, "mode", None, None),
        P("chan", None, "mode", None, None),
        P("chan", None, None, "mode", None),
        P("chan", None, None, "mode", None),
        P("chan", None),
        P(),
        P(),
        P(),
    )
    out_specs = (
        P("chan", None, "mode", None, None),
        P("chan", None, None, "mode", None),
        P("chan", None, None, "mode", None),
    )
    return jax.shard_map(shards, mesh=mesh, in_specs=in_specs, out_specs=out_specs, check_vma=False)
```
